32 devices in a mesh: dp: 2 (over y), seq: 16 (over z, x, core).
Axes of the slice: x: 2, y: 2, z: 4, core: 2. Of those that a mesh axis runs over, the one named last changes fastest.
Arguments:
- tokens: bfloat16 [2, 4096, 768], P('dp', 'seq'), may hold values from -6 to 6
- segment_ids: int32 [2, 4096], P('dp', 'seq'), may hold values from 0 to 7, never falling along the last dimension, each value on 1 to 2048 neighbouring positions
- features: bfloat16 [12, 64, 256], replicated, may hold values from -6 to 6
- query_weight: bfloat16 [768, 768], replicated, may hold values from -0.15625 to 0.15625
- key_weight: bfloat16 [768, 768], replicated, may hold values from -0.15625 to 0.15625
- value_weight: bfloat16 [768, 768], replicated, may hold values from -0.21875 to 0.21875
- out_weight: bfloat16 [768, 768], replicated, may hold values from -0.875 to 0.875
- up_weight: bfloat16 [768, 3072], replicated, may hold values from -0.21875 to 0.21875
- down_weight: bfloat16 [3072, 768], replicated, may hold values from -0.109375 to 0.109375
- first_gain: float32 [768], replicated, may hold values from 0.1 to 1.9
- first_bias: float32 [768], replicated, may hold values from -3 to 3
- second_gain: float32 [768], replicated, may hold values from 0.1 to 1.9
- second_bias: float32 [768], replicated, may hold values from -3 to 3
- cotangent: bfloat16 [2, 4096, 768], P('dp', 'seq'), may hold values from -6 to 6
Outputs:
- output: bfloat16 [2, 4096, 768], P('dp', 'seq')
- grad_tokens: bfloat16 [2, 4096, 768], P('dp', 'seq')
- grad_query: float32 [768, 768], replicated
- grad_key: float32 [768, 768], replicated
- grad_value: float32 [768, 768], replicated
- grad_out: float32 [768, 768], replicated
- grad_up: float32 [768, 3072], replicated
- grad_down: float32 [3072, 768], replicated
- grad_first_gain: float32 [768], replicated
- grad_first_bias: float32 [768], replicated
- grad_second_gain: float32 [768], replicated
- grad_second_bias: float32 [768], replicated
The draws below stay inside these ranges and needn't reach their ends.
Inputs may be any that keep to these rules, and one draw needn't show every extreme that they name: `segment_ids`: in each row the ids never fall, every id from 0 to 7 occurs, each on 1 to 2048 positions, and one on exactly 2048.
All inputs are finite; a program needn't handle non-finite values.
Results may differ from the reference program's by a relative error of at most 0.02.
Values sent between devices are 32-bit elements; how exact they have to be, the bound alone decides.
No kernel may reach another device: no remote copies, remote signals or barrier semaphores. Data moves between devices by JAX's collectives and lax.ppermute only.
A program may use at most 320 MiB of HBM per device.

```python
import math
import jax
import jax.numpy as jnp
import numpy as np
from jax import lax

D = 768
HEADS = 12
HD = 64
FF = 3072
FEATS = 256
SEGS = 8
LEN = 4096
ROWS = 2
SEG_MOST = 2048


def spiked(values, own_key, source, target, shards_of, factor):
    owner, partner = [(jnp.arange(values.shape[position]) // (values.shape[position] // shards_of)).reshape([-1 if axis == position else 1 for axis in range(values.ndim)]) for position in (source, target)]
    chosen = jax.random.permutation(own_key, shards_of)[partner]
    strong = (owner == chosen) | (owner == (partner + shards_of // 2) % shards_of)
    return jnp.where(strong, factor * values, values)


def shard_levels(stream_key, shape, split, low, largest):
    loudness, own = 1.0, jax.random.fold_in(stream_key, 6)
    for axis_at, parts in split:
        draws = jnp.exp(jax.random.uniform(jax.random.fold_in(own, axis_at), (parts,), jnp.float32, low / len(split), largest / len(split)))
        loudness = loudness * jnp.repeat(draws, shape[axis_at] // parts).reshape([-1 if axis == axis_at else 1 for axis in range(len(shape))])
    return loudness


def split_up(number_of, total, bound, slope):
    loads = [(1 << 20) // math.isqrt(rank ** slope) + 1 for rank in range(2, number_of + 1)]
    rest, counts = total - bound - (number_of - 1), [1] * (number_of - 1)
    while rest > 0:
        candidates = [i for i in range(number_of - 1) if counts[i] < bound]
        whole, left = sum([loads[i] for i in candidates]), rest
        for i in candidates:
            more = min(bound - counts[i], max(1, left * loads[i] // whole), rest)
            counts[i] = counts[i] + more
            rest = rest - more
    return np.array([bound] + counts)


def ragged(rng, amount, total, bound, lean):
    if amount == 2:
        one = jax.random.randint(rng, (), max(1, total - bound), min(bound, total - 1) + 1)
        return jnp.stack([one, total - one])
    lengths = jnp.asarray(split_up(amount, total, bound, lean), jnp.int32)
    pairs = (amount - 1) // 2
    source_of, taker = lengths[1:1 + 2 * pairs:2], lengths[2:2 + 2 * pairs:2]
    slack = jnp.minimum(source_of - 1, bound - taker)
    moved = jax.random.randint(jax.random.fold_in(rng, 1), (pairs,), 0, 1 << 20) % (slack + 1)
    lengths = lengths.at[1:1 + 2 * pairs:2].set(source_of - moved).at[2:2 + 2 * pairs:2].set(taker + moved)
    return lengths[jax.random.permutation(jax.random.fold_in(rng, 2), amount)]


def normal_values(rng, dims, spread, limit, split=(), kind=jnp.bfloat16):
    gain = shard_levels(rng, dims, split, -0.22, 0.18) if split else 1.0
    drawn = jax.random.normal(rng, dims, jnp.float32) * spread * gain
    return jnp.minimum(jnp.maximum(drawn, -limit), limit).astype(kind)


def heavy_noise(rng, extent, deviation, limit, split, heavy, kind=jnp.bfloat16):
    values = deviation * jax.random.normal(rng, extent, jnp.float32)
    if split:
        values = values * shard_levels(rng, extent, split, -0.22, 0.18)
    return jnp.clip(spiked(values, jax.random.fold_in(rng, 3), *heavy), -limit, limit).astype(kind)


def setup_inputs(seed: int = 0) -> dict:
    splits = jax.random.split(jax.random.key(seed), 15)
    return {
        "tokens": normal_values(splits[0], (ROWS, LEN, D), 1.0, 6.0, ((0, 2), (1, 16))),
        "segment_ids": jax.vmap(lambda own: jnp.searchsorted(jnp.cumsum(ragged(own, SEGS, LEN, SEG_MOST, 2)), jnp.arange(LEN), side="right"))(jax.random.split(splits[1], ROWS)).reshape((ROWS, LEN)).astype(jnp.int32),
        "features": normal_values(splits[2], (HEADS, HD, FEATS), 1.0, 6.0),
        "query_weight": normal_values(splits[3], (D, D), (2 * D) ** -0.5, 0.15625),
        "key_weight": normal_values(splits[4], (D, D), (2 * D) ** -0.5, 0.15625),
        "value_weight": normal_values(splits[5], (D, D), D ** -0.5, 0.21875),
        "out_weight": normal_values(splits[6], (D, D), (D // 16) ** -0.5, 0.875),
        "up_weight": normal_values(splits[7], (D, FF), D ** -0.5, 0.21875),
        "down_weight": normal_values(splits[8], (FF, D), FF ** -0.5, 0.109375),
        "first_gain": jnp.clip(1.0 + 0.18 * jax.random.normal(splits[9], (D,), jnp.float32), 0.1, 1.9),
        "first_bias": normal_values(splits[10], (D,), 0.5, 3.0, (), jnp.float32),
        "second_gain": jnp.clip(1.0 + 0.18 * jax.random.normal(splits[11], (D,), jnp.float32), 0.1, 1.9),
        "second_bias": normal_values(splits[12], (D,), 0.5, 3.0, (), jnp.float32),
        "cotangent": heavy_noise(splits[13], (ROWS, LEN, D), 1.0, 6.0, ((0, 2), (1, 16)), (1, 2, 16, 2.0)),
    }


EPSILON = 1e-06
HIGHEST = lax.Precision.HIGHEST

@jax.custom_vjp
def low(v):
    return lax.optimization_barrier(v.astype(jnp.bfloat16)).astype(jnp.float32)

@jax.custom_vjp
def low_back(v):
    return v

def low_keep(v):
    return (low(v), None)

def low_pass(kept, grad):
    return (grad,)

def back_keep(v):
    return (v, None)

def back_low(kept, grad):
    return (low(grad),)
low.defvjp(low_keep, low_pass)
low_back.defvjp(back_keep, back_low)

def layer_norm(hidden, norm_gain, norm_bias):
    row_mean = lax.optimization_barrier(jnp.mean(hidden, -1, keepdims=True))
    centered = hidden - row_mean
    variance = lax.optimization_barrier(jnp.mean(centered * centered, -1, keepdims=True))
    return centered * lax.rsqrt(variance + EPSILON) * norm_gain + norm_bias

def feature_map(projected, features):
    rounded = low(low_back(projected))
    inner_u = low_back(jnp.einsum('the,hem->thm', rounded, features, precision=HIGHEST))
    square = lax.optimization_barrier(jnp.sum(rounded * rounded, -1, keepdims=True))
    return low(jnp.exp(inner_u * HD ** (-0.25) - 0.5 * HD ** (-0.5) * square) * FEATS ** (-0.5))

def forward_row(x_row, onehot, features, query_weight, key_weight, value_weight, out_weight, up_weight, down_weight, first_gain, first_bias, second_gain, second_bias):
    positions = x_row.shape[0]

    def split_heads(weight):
        return jnp.dot(x_row, weight, precision=HIGHEST).reshape(positions, HEADS, HD)
    feat_q = feature_map(split_heads(query_weight), features)
    feat_k = feature_map(split_heads(key_weight), features)
    values_b = low(low_back(split_heads(value_weight)))
    numer = jnp.zeros((positions, HEADS, HD), jnp.float32)
    denom = jnp.zeros((positions, HEADS), jnp.float32)
    for segment in range(SEGS):
        select = onehot[:, segment][:, None, None]
        masked_k = feat_k * select
        kv_sum = jnp.einsum('thm,the->hme', masked_k, values_b, precision=HIGHEST)
        z_sum = lax.optimization_barrier(jnp.sum(masked_k, 0))
        kv_low = low(low_back(kv_sum))
        numer = numer + select * jnp.einsum('thm,hme->the', feat_q, kv_low, precision=HIGHEST)
        denom = denom + select[:, :, 0] * jnp.einsum('thm,hm->th', feat_q, z_sum, precision=HIGHEST)
    numer = low_back(numer)
    attention = low((numer / denom[:, :, None]).reshape(positions, D))
    hidden_one = x_row + low_back(jnp.dot(attention, out_weight, precision=HIGHEST))
    normed_one = layer_norm(hidden_one, first_gain, first_bias)
    inner_f = low_back(jnp.dot(low(normed_one), up_weight, precision=HIGHEST))
    activated = low(jax.nn.gelu(inner_f, approximate=False))
    branch = low_back(jnp.dot(activated, down_weight, precision=HIGHEST))
    return layer_norm(normed_one + branch, second_gain, second_bias)

def reference(tokens, segment_ids, features, query_weight, key_weight, value_weight, out_weight, up_weight, down_weight, first_gain, first_bias, second_gain, second_bias, cotangent):
    weights = (query_weight.astype(jnp.float32), key_weight.astype(jnp.float32), value_weight.astype(jnp.float32), out_weight.astype(jnp.float32), up_weight.astype(jnp.float32), down_weight.astype(jnp.float32), first_gain.astype(jnp.float32), first_bias.astype(jnp.float32), second_gain.astype(jnp.float32), second_bias.astype(jnp.float32))
    feat_mats = features.astype(jnp.float32)
    labels = jnp.arange(SEGS, dtype=jnp.int32)

    def one_row(totals, row_data):
        x_row, seg_row, cot_row = row_data
        onehot = (seg_row[:, None] == labels[None, :]).astype(jnp.float32)

        def run_row(x_in, *params):
            return forward_row(x_in, onehot, feat_mats, *params)
        result, pull_back = jax.vjp(run_row, x_row.astype(jnp.float32), *weights)
        grads = pull_back(cot_row.astype(jnp.float32))
        totals = tuple((acc + new for acc, new in zip(totals, grads[1:])))
        return (totals, (result.astype(jnp.bfloat16), grads[0].astype(jnp.bfloat16)))
    start = tuple((jnp.zeros_like(w) for w in weights))
    totals, (outputs, grad_in) = lax.scan(one_row, start, (tokens, segment_ids, cotangent))
    return (outputs, grad_in, totals[0], totals[1], totals[2], totals[3], totals[4], totals[5], totals[6], totals[7], totals[8], totals[9])
```

```python
from functools import partial

import jax
import jax.numpy as jnp
from jax import lax
from jax.experimental import pallas as pl
from jax.experimental.pallas import tpu as pltpu
from jax.sharding import PartitionSpec as P

SEG_MOST = 2048
EPSILON = 1e-06
QUAD = 4
NT = (((1,), (1,)), ((), ()))
NN = (((1,), (0,)), ((), ()))
TN = (((0,), (0,)), ((), ()))


def mxu(a, b, dims):
    return lax.dot_general(a, b, dims, preferred_element_type=jnp.float32)


def norm_forward(hidden, norm_gain, norm_bias):
    row_mean = jnp.mean(hidden, -1, keepdims=True)
    centered = hidden - row_mean
    variance = jnp.mean(centered * centered, -1, keepdims=True)
    inv_std = lax.rsqrt(variance + EPSILON)
    normed = centered * inv_std
    return (normed * norm_gain + norm_bias, normed, inv_std)


def norm_backward(upstream, normed, inv_std, norm_gain):
    scaled = upstream * norm_gain
    grad_hidden = inv_std * (
        scaled
        - jnp.mean(scaled, -1, keepdims=True)
        - normed * jnp.mean(scaled * normed, -1, keepdims=True)
    )
    return (grad_hidden, jnp.sum(upstream * normed, 0), jnp.sum(upstream, 0))


def features_of(rows, feats):
    head_dim, count = feats.shape
    wide = rows.astype(jnp.float32)
    square = jnp.sum(wide * wide, -1, keepdims=True)
    inner = mxu(rows, feats, NN)
    return jnp.exp(inner * head_dim ** (-0.25) - 0.5 * head_dim ** (-0.5) * square) * count ** (-0.5)


def features_back(weighted, rows, feats):
    head_dim = feats.shape[0]
    inner = (weighted * head_dim ** (-0.25)).astype(jnp.bfloat16)
    grad = mxu(inner, feats, NT)
    total = jnp.sum(weighted, -1, keepdims=True)
    return (grad - head_dim ** (-0.5) * rows.astype(jnp.float32) * total).astype(jnp.bfloat16)


class Plan:
    def __init__(self, heads, head_dim):
        self.heads, self.dim = heads, head_dim
        self.each = heads // QUAD
        self.block = self.each * head_dim + 8
        self.rows = QUAD * self.block

    def kv_row(self, head):
        return (head // self.each) * self.block + (head % self.each) * self.dim

    def z_row(self, head):
        return (head // self.each) * self.block + self.each * self.dim + head % self.each

    @property
    def first_row(self):
        return self.each * self.dim + self.each

    @property
    def last_row(self):
        return self.each * self.dim + self.each + 1


def put_state(plan, state_ref, head, pair_sum, z_lead, z_tail):
    at = pl.multiple_of(plan.kv_row(head), 8)
    state_ref[0, pl.ds(at, plan.dim), :] = pair_sum[: plan.dim]
    state_ref[1, pl.ds(at, plan.dim), :] = pair_sum[plan.dim :]
    z_at = plan.z_row(head)
    state_ref[0, pl.ds(z_at, 1), :] = z_lead
    state_ref[1, pl.ds(z_at, 1), :] = z_tail


def put_ids(plan, state_ref, seg_col):
    wide = state_ref.shape[2]
    length = seg_col.shape[0]
    first = jnp.broadcast_to(seg_col[0:1, :], (1, wide))
    last = jnp.broadcast_to(seg_col[length - 1 : length, :], (1, wide))
    for quarter in range(QUAD):
        base = quarter * plan.block
        state_ref[:, base + plan.block - 8 : base + plan.block, :] = jnp.zeros((2, 8, wide), jnp.float32)
        for side in range(2):
            state_ref[side, base + plan.first_row : base + plan.first_row + 1, :] = first
            state_ref[side, base + plan.last_row : base + plan.last_row + 1, :] = last


def get_carry(plan, carry_ref, head):
    at = pl.multiple_of(plan.kv_row(head), 8)
    z_at = plan.z_row(head)
    from_before = carry_ref[0, pl.ds(at, plan.dim), :]
    from_behind = carry_ref[1, pl.ds(at, plan.dim), :]
    both = jnp.concatenate([from_before, from_behind], 0).astype(jnp.bfloat16)
    return both, carry_ref[0, pl.ds(z_at, 1), :], carry_ref[1, pl.ds(z_at, 1), :]


def two_sided(rows, on_first, on_last):
    zero = jnp.zeros_like(rows)
    return jnp.concatenate([jnp.where(on_first, rows, zero), jnp.where(on_last, rows, zero)], 1)


def edges(seg_col):
    length = seg_col.shape[0]
    return seg_col == seg_col[0:1, :], seg_col == seg_col[length - 1 : length, :]


def project_kernel(plan, x_ref, wq_ref, wk_ref, wv_ref, feats_ref, seg_ref, q_ref, k_ref, v_ref, state_ref):
    step = pl.program_id(0)
    seg_col = seg_ref[...]

    @pl.when(step == 0)
    def _():
        put_ids(plan, state_ref, seg_col)

    x = x_ref[...]
    q_ref[...] = mxu(x, wq_ref[...], NN).astype(jnp.bfloat16)
    keys = mxu(x, wk_ref[...], NN).astype(jnp.bfloat16)
    values = mxu(x, wv_ref[...], NN).astype(jnp.bfloat16)
    k_ref[...] = keys
    v_ref[...] = values
    on_first, on_last = edges(seg_col)
    for i in range(2):
        lanes = slice(i * plan.dim, (i + 1) * plan.dim)
        feat_k = features_of(keys[:, lanes], feats_ref[i]).astype(jnp.bfloat16)
        sums = mxu(two_sided(values[:, lanes], on_first, on_last), feat_k, TN)
        wide = feat_k.astype(jnp.float32)
        z_lead = jnp.sum(jnp.where(on_first, wide, 0.0), 0, keepdims=True)
        z_tail = jnp.sum(jnp.where(on_last, wide, 0.0), 0, keepdims=True)
        put_state(plan, state_ref, 2 * step + i, sums, z_lead, z_tail)


def attend_kernel(plan, q_ref, k_ref, v_ref, feats_ref, seg_ref, row_ref, carry_ref, att_ref, attb_ref, den_ref):
    step = pl.program_id(0)
    seg_col = seg_ref[...]
    same = seg_col == row_ref[...]
    on_first, on_last = edges(seg_col)
    for i in range(2):
        lanes = slice(i * plan.dim, (i + 1) * plan.dim)
        fq = features_of(q_ref[:, lanes], feats_ref[i]).astype(jnp.bfloat16)
        fk = features_of(k_ref[:, lanes], feats_ref[i]).astype(jnp.bfloat16)
        both, z_before, z_behind = get_carry(plan, carry_ref, 2 * step + i)
        z_rows = jnp.where(on_first, z_before, 0.0) + jnp.where(on_last, z_behind, 0.0)
        scores = jnp.where(same, mxu(fq, fk, NT), 0.0)
        reach = mxu(fq, both, NT)
        numer = (
            mxu(scores.astype(jnp.bfloat16), v_ref[:, lanes], NN)
            + jnp.where(on_first, reach[:, : plan.dim], 0.0)
            + jnp.where(on_last, reach[:, plan.dim :], 0.0)
        )
        denom = jnp.sum(scores, -1, keepdims=True) + jnp.sum(
            fq.astype(jnp.float32) * z_rows, -1, keepdims=True
        )
        attention = numer / denom
        att_ref[:, lanes] = attention
        attb_ref[:, lanes] = attention.astype(jnp.bfloat16)
        den_ref[:, lanes] = jnp.broadcast_to(denom, attention.shape)


def pull_head(grad, attention, denom):
    grad_numer = (grad / denom).astype(jnp.bfloat16)
    grad_denom = -jnp.sum(grad * attention, -1, keepdims=True) / denom[:, :1]
    return grad_numer, grad_denom


def query_kernel(
    plan, q_ref, k_ref, v_ref, feats_ref, seg_ref, row_ref, carry_ref, grad_ref, att_ref, den_ref, dq_ref, state_ref
):
    step = pl.program_id(0)
    seg_col = seg_ref[...]

    @pl.when(step == 0)
    def _():
        put_ids(plan, state_ref, seg_col)

    same = seg_col == row_ref[...]
    on_first, on_last = edges(seg_col)
    for i in range(2):
        lanes = slice(i * plan.dim, (i + 1) * plan.dim)
        rows = q_ref[:, lanes]
        feat_q = features_of(rows, feats_ref[i])
        fq = feat_q.astype(jnp.bfloat16)
        fk = features_of(k_ref[:, lanes], feats_ref[i]).astype(jnp.bfloat16)
        both, z_before, z_behind = get_carry(plan, carry_ref, 2 * step + i)
        z_rows = jnp.where(on_first, z_before, 0.0) + jnp.where(on_last, z_behind, 0.0)
        grad_numer, grad_denom = pull_head(grad_ref[:, lanes], att_ref[:, lanes], den_ref[:, lanes])
        pulled = mxu(grad_numer, v_ref[:, lanes], NT) + grad_denom
        pulled = jnp.where(same, pulled, 0.0).astype(jnp.bfloat16)
        sides = two_sided(grad_numer, on_first, on_last)
        grad_feat = mxu(pulled, fk, NN) + mxu(sides, both, NN) + grad_denom * z_rows
        dq_ref[:, lanes] = features_back(grad_feat * feat_q, rows, feats_ref[i])
        sums = mxu(sides, fq, TN)
        scaled = fq.astype(jnp.float32) * grad_denom
        z_lead = jnp.sum(jnp.where(on_first, scaled, 0.0), 0, keepdims=True)
        z_tail = jnp.sum(jnp.where(on_last, scaled, 0.0), 0, keepdims=True)
        put_state(plan, state_ref, 2 * step + i, sums, z_lead, z_tail)


def key_kernel(
    plan, q_ref, k_ref, v_ref, feats_ref, seg_ref, row_ref, carry_ref, grad_ref, att_ref, den_ref, dk_ref, dv_ref
):
    step = pl.program_id(0)
    seg_col = seg_ref[...]
    same = seg_col == row_ref[...]
    on_first, on_last = edges(seg_col)
    for i in range(2):
        lanes = slice(i * plan.dim, (i + 1) * plan.dim)
        rows = k_ref[:, lanes]
        values = v_ref[:, lanes]
        fq = features_of(q_ref[:, lanes], feats_ref[i]).astype(jnp.bfloat16)
        feat_k = features_of(rows, feats_ref[i])
        fk = feat_k.astype(jnp.bfloat16)
        both, z_before, z_behind = get_carry(plan, carry_ref, 2 * step + i)
        grad_numer, grad_denom = pull_head(grad_ref[:, lanes], att_ref[:, lanes], den_ref[:, lanes])
        pulled = mxu(grad_numer, values, NT) + grad_denom
        pulled = jnp.where(same, pulled, 0.0).astype(jnp.bfloat16)
        scores = jnp.where(same, mxu(fk, fq, NT), 0.0).astype(jnp.bfloat16)
        grad_feat = (
            mxu(pulled, fq, TN)
            + mxu(two_sided(values, on_first, on_last), both, NN)
            + jnp.where(on_first, z_before, 0.0)
            + jnp.where(on_last, z_behind, 0.0)
        )
        reach = mxu(fk, both, NT)
        grad_values = (
            mxu(scores, grad_numer, NN)
            + jnp.where(on_first, reach[:, : plan.dim], 0.0)
            + jnp.where(on_last, reach[:, plan.dim :], 0.0)
        )
        dv_ref[:, lanes] = grad_values.astype(jnp.bfloat16)
        dk_ref[:, lanes] = features_back(grad_feat * feat_k, rows, feats_ref[i])


def exchange(plan, state, axis, row_len):
    count, place = lax.axis_size(axis), lax.axis_index(axis)
    block = plan.block

    def ids(part):
        first = part[0, plan.first_row, 0]
        last = part[0, plan.last_row, 0]
        return first, last

    def swap(part, bit):
        return lax.ppermute(part, axis, [(i, i ^ bit) for i in range(count)])

    def up(part, bit):
        high = (place // bit) % 2
        half = part.shape[1] // 2
        mine = lax.dynamic_slice_in_dim(part, high * half, half, 1)
        theirs = swap(lax.dynamic_slice_in_dim(part, (1 - high) * half, half, 1), bit)
        low = jnp.where(high == 0, mine, theirs)
        upper = jnp.where(high == 0, theirs, mine)
        (first_low, last_low), (first_up, last_up) = ids(low), ids(upper)
        lead = low[0] + jnp.where(first_low == first_up, upper[0], 0.0)
        tail = upper[1] + jnp.where(last_low == last_up, low[1], 0.0)
        return lead, tail, first_low, last_up, (low, upper)

    def mark(plan, lead, tail, first, last):
        rows = lax.broadcasted_iota(jnp.int32, (lead.shape[0], 1), 0) % block
        both = jnp.stack([lead, tail])
        both = jnp.where((rows == plan.first_row)[None], first, both)
        return jnp.where((rows == plan.last_row)[None], last, both)

    def down(carry, first, last, children, bit):
        low, upper = children
        high = (place // bit) % 2
        (first_low, last_low), (first_up, last_up) = ids(low), ids(upper)
        joined = last_low == first_up
        low_carry = jnp.stack(
            [carry[0], jnp.where(joined, upper[0], 0.0) + jnp.where(last_low == last, carry[1], 0.0)]
        )
        up_carry = jnp.stack(
            [jnp.where(joined, low[1], 0.0) + jnp.where(first_up == first, carry[0], 0.0), carry[1]]
        )
        mine = jnp.where(high == 0, low_carry, up_carry)
        theirs = swap(jnp.where(high == 0, up_carry, low_carry), bit)
        return jnp.concatenate(
            [jnp.where(high == 0, mine, theirs), jnp.where(high == 0, theirs, mine)], 1
        )

    lead, tail, first1, last1, children1 = up(state, 1)
    chip = mark(plan, lead, tail, first1, last1)
    lead, tail, first2, last2, children2 = up(chip, 2)
    quad = mark(plan, lead, tail, first2, last2)
    quads = count // QUAD
    reach = min(quads - 1, -(-SEG_MOST // (QUAD * row_len)))
    here = place // QUAD
    before = jnp.zeros_like(lead)
    behind = jnp.zeros_like(lead)
    for far in range(1, reach + 1):
        hop = far * QUAD
        lower = lax.ppermute(quad[1], axis, [(i, i + hop) for i in range(count - hop)])
        higher = lax.ppermute(quad[0], axis, [(i + hop, i) for i in range(count - hop)])
        low_last = lower[plan.last_row, 0]
        high_first = higher[plan.first_row, 0]
        before = before + jnp.where((here >= far) & (low_last == first2), lower, 0.0)
        behind = behind + jnp.where((here + far < quads) & (high_first == last2), higher, 0.0)
    carry = jnp.stack([before, behind])
    carry = down(carry, first2, last2, children2, 2)
    return down(carry, first1, last1, children1, 1)


def body(
    tokens,
    segment_ids,
    features,
    query_weight,
    key_weight,
    value_weight,
    out_weight,
    up_weight,
    down_weight,
    first_gain,
    first_bias,
    second_gain,
    second_bias,
    cotangent,
):
    row_count, row_len, width_d = tokens.shape
    head_count, head_dim, feat_count = features.shape
    plan = Plan(head_count, head_dim)
    x = tokens.reshape(row_count * row_len, width_d)
    seg = segment_ids.astype(jnp.float32)
    steps = head_count // 2
    lanes = 2 * head_dim

    pair = pl.BlockSpec((row_len, lanes), lambda p: (0, p))
    weight = pl.BlockSpec((width_d, lanes), lambda p: (0, p))
    feats = pl.BlockSpec((2, head_dim, feat_count), lambda p: (p, 0, 0))
    whole = lambda shape: pl.BlockSpec(shape, lambda p: (0,) * len(shape))
    col, row = whole((row_len, 1)), whole((1, row_len))
    state_shape = (2, plan.rows, feat_count)
    state = whole(state_shape)
    tall = lambda dtype: jax.ShapeDtypeStruct((row_len, width_d), dtype)
    state_out = jax.ShapeDtypeStruct(state_shape, jnp.float32)
    bf16, f32 = jnp.bfloat16, jnp.float32

    def call(kernel, ins, outs, shapes):
        return pl.pallas_call(
            partial(kernel, plan),
            grid=(steps,),
            in_specs=ins,
            out_specs=outs,
            out_shape=shapes,
            name=kernel.__name__,
            compiler_params=pltpu.CompilerParams(dimension_semantics=("arbitrary",)),
        )

    def per_row(work, *arrays):
        cut = lambda a, r: a[r * row_len : (r + 1) * row_len]
        done = [work(r, *[cut(a, r) for a in arrays]) for r in range(row_count)]
        if row_count == 1:
            return done[0]
        return tuple(jnp.concatenate(parts) for parts in zip(*done))

    kept = {}

    def attend(r, x_row):
        seg_col, seg_row = seg[r].reshape(row_len, 1), seg[r].reshape(1, row_len)
        queries, keys, values, own = call(
            project_kernel,
            [whole((row_len, width_d)), weight, weight, weight, feats, col],
            [pair, pair, pair, state],
            [tall(bf16), tall(bf16), tall(bf16), state_out],
        )(x_row, query_weight, key_weight, value_weight, features, seg_col)
        carry = exchange(plan, own, "seq", row_len)
        attention, attention_b, denom = call(
            attend_kernel,
            [pair, pair, pair, feats, col, row, state],
            [pair, pair, pair],
            [tall(f32), tall(bf16), tall(f32)],
        )(queries, keys, values, features, seg_col, seg_row, carry)
        kept[r] = (queries, keys, values, features, seg_col, seg_row, carry, attention, denom)
        return (attention_b,)

    (attention_b,) = per_row(attend, x)

    hidden_one = x.astype(f32) + jnp.dot(attention_b, out_weight, preferred_element_type=f32)
    normed_one, unit_one, inv_one = norm_forward(hidden_one, first_gain, first_bias)
    normed_one_b = normed_one.astype(bf16)
    inner_f = jnp.dot(normed_one_b, up_weight, preferred_element_type=f32)
    activated, gelu_pull = jax.vjp(partial(jax.nn.gelu, approximate=False), inner_f)
    activated_b = activated.astype(bf16)
    hidden_two = normed_one + jnp.dot(activated_b, down_weight, preferred_element_type=f32)
    result, unit_two, inv_two = norm_forward(hidden_two, second_gain, second_bias)
    upstream = cotangent.reshape(row_count * row_len, width_d).astype(f32)
    grad_two, grad_gain_two, grad_bias_two = norm_backward(upstream, unit_two, inv_two, second_gain)
    grad_branch = grad_two.astype(bf16)
    grad_down_w = mxu(activated_b, grad_branch, TN)
    (grad_inner,) = gelu_pull(mxu(grad_branch, down_weight, NT))
    grad_inner_b = grad_inner.astype(bf16)
    grad_up_w = mxu(normed_one_b, grad_inner_b, TN)
    grad_normed = grad_two + mxu(grad_inner_b, up_weight, NT)
    grad_one, grad_gain_one, grad_bias_one = norm_backward(grad_normed, unit_one, inv_one, first_gain)
    grad_attn_out = grad_one.astype(bf16)
    grad_out_w = mxu(attention_b, grad_attn_out, TN)
    grad_attention = mxu(grad_attn_out, out_weight, NT)

    def pull_back(r, grad_row):
        queries, keys, values, _, seg_col, seg_row, carry, attention, denom = kept[r]
        back_ins = [pair, pair, pair, feats, col, row, state, pair, pair, pair]
        first = (queries, keys, values, features, seg_col, seg_row)
        then = (grad_row, attention, denom)
        grad_q, own = call(query_kernel, back_ins, [pair, state], [tall(bf16), state_out])(*first, carry, *then)
        carry_back = exchange(plan, own, "seq", row_len)
        grad_k, grad_v = call(key_kernel, back_ins, [pair, pair], [tall(bf16), tall(bf16)])(
            *first, carry_back, *then
        )
        return grad_q, grad_k, grad_v

    grad_q, grad_k, grad_v = per_row(pull_back, grad_attention)
    grad_query_w = mxu(x, grad_q, TN)
    grad_key_w = mxu(x, grad_k, TN)
    grad_value_w = mxu(x, grad_v, TN)
    grad_input = (
        grad_one
        + mxu(grad_q, query_weight, NT)
        + mxu(grad_k, key_weight, NT)
        + mxu(grad_v, value_weight, NT)
    )
    grads = (
        grad_query_w,
        grad_key_w,
        grad_value_w,
        grad_out_w,
        grad_up_w,
        grad_down_w,
        grad_gain_one,
        grad_bias_one,
        grad_gain_two,
        grad_bias_two,
    )
    grads = lax.psum(grads, ("dp", "seq"))
    shape = (row_count, row_len, width_d)
    return (result.astype(bf16).reshape(shape), grad_input.astype(bf16).reshape(shape)) + tuple(grads)


def solution(mesh):
    tokens = P("dp", "seq", None)
    return jax.shard_map(
        body,
        mesh=mesh,
        in_specs=(tokens, P("dp", "seq")) + (P(),) * 11 + (tokens,),
        out_specs=(tokens, tokens) + (P(),) * 10,
        check_vma=False,
    )
```
